32 devices in a mesh: shot: 32 (over z, y, x, core), freq: 1.
Axes of the slice: x: 2, y: 2, z: 4, core: 2. Of those that a mesh axis runs over, the one named last changes fastest.
Arguments:
- data: bfloat16 [2, 64, 128, 128], P(None, 'freq', 'shot')
- aperture: int32 [128, 64], P('shot'), may hold values from -1 to 127, as said below
- ops: bfloat16 [8, 64, 64], replicated, may hold values from -0.75 to 0.75
- cable_ops: int32 [2], replicated, may hold values from 0 to 7
Outputs:
- multiples: bfloat16 [2, 64, 128, 128], P(None, 'freq', 'shot')
The draws below stay inside these ranges and needn't reach their ends.
Inputs may be any that keep to these rules, and one draw needn't show every extreme that they name: `aperture`: each shot's list holds 1 to 64 distinct surface points first, then -1 padding; some shot's list is full.
All inputs are finite; a program needn't handle non-finite values.
Results may differ from the reference program's by a relative error of at most 0.0004.
Values may be sent and summed in bfloat16 or wider, within the bound.
A program may use at most 64 MiB of HBM per device.

```python
import jax
import jax.numpy as jnp
from jax import lax

APER = 64
CAB = 64
NOPS = 8
N = 128
FREQS = 64
NCAB = 2


def draw_data(key, part):
    first, second = jax.random.split(key, 2)
    shape = (2, FREQS, N, N)
    position = jnp.arange(FREQS, dtype=jnp.float32) / max(FREQS - 1, 1)
    base = jnp.clip(jax.random.normal(first, shape, jnp.float32), -6.0, 6.0)
    ramp = 1.0 + 2.0 * position
    shot_scale = jnp.exp(jax.random.uniform(second, (N,), jnp.float32, 0.0, 2.3))
    values = base * ramp[None, :, None, None] * shot_scale[None, None, :, None]
    return values.astype(jnp.bfloat16)


def draw_aperture(key, part):
    first, second = jax.random.split(key, 2)
    row_keys = jax.random.split(first, N)
    orders = jax.vmap(lambda one_key: jax.random.permutation(one_key, N))(row_keys)[:, :APER].astype(jnp.int32)
    lengths = jax.random.randint(second, (N,), max(APER // 4, 1), APER + 1).astype(jnp.int32)
    lengths = lengths.at[0].set(APER)
    slots = jnp.arange(APER, dtype=jnp.int32)
    return jnp.where(slots[None, :] < lengths[:, None], orders, -1).astype(jnp.int32)


def centred(key, extent, scale, reach, kind=jnp.bfloat16):
    result = jax.random.normal(key, extent, jnp.float32) * scale
    return jnp.minimum(jnp.maximum(result, -reach), reach).astype(kind)


def setup_inputs(seed: int = 0) -> dict:
    key_list = jax.random.split(jax.random.key(seed), 5)
    data = draw_data(jax.random.fold_in(key_list[4], 71), 0)
    aperture = draw_aperture(jax.random.fold_in(key_list[4], 71), 0)
    ops = centred(key_list[2], (NOPS, CAB, CAB), CAB ** -0.5, 0.75)
    cable_ops = jax.random.randint(key_list[3], (NCAB,), 0, NOPS).astype(jnp.int32)
    return {"data": data, "aperture": aperture, "ops": ops, "cable_ops": cable_ops}


def reference(data, aperture, ops, cable_ops):
    highest_value = lax.Precision.HIGHEST
    total = data.shape[3]
    bands = data.shape[1]
    surface = jnp.arange(total, dtype=jnp.int32)
    mask = jnp.any(aperture[:, :, None] == surface[None, None, :], axis=1).astype(jnp.float32)
    values = data.astype(jnp.float32)
    masked_wavefield = values * mask[None, None, :, :]
    chosen = ops[cable_ops].astype(jnp.float32)
    cables = total // CAB
    filtered_traces = jnp.einsum('pfkci,cij->pfkcj', values.reshape(2, bands, total, cables, CAB), chosen, precision=highest_value)
    filtered_traces = filtered_traces.reshape(2, bands, total, total)
    real_part = jnp.einsum('jpy,jyu->jpu', masked_wavefield[0], filtered_traces[0], precision=highest_value) - jnp.einsum('jpy,jyu->jpu', masked_wavefield[1], filtered_traces[1], precision=highest_value)
    imaginary_part = jnp.einsum('jpy,jyu->jpu', masked_wavefield[0], filtered_traces[1], precision=highest_value) + jnp.einsum('jpy,jyu->jpu', masked_wavefield[1], filtered_traces[0], precision=highest_value)
    predicted = jnp.stack([real_part, imaginary_part])
    energy = lax.optimization_barrier(jnp.sum(predicted * predicted, axis=(0, 1, 3)))
    scale = lax.rsqrt(energy / (2.0 * bands * total) + 1e-06)
    return (predicted * scale[None, None, :, None]).astype(jnp.bfloat16)
```

```python
import functools

import jax
import jax.numpy as jnp
from jax import lax
from jax.experimental import pallas as pl
from jax.experimental.pallas import tpu as pltpu
from jax.sharding import PartitionSpec as P

MESH = pl.DeviceIdType.MESH

def kernel(n, sizes, finish, data, aperture, ops, cable_ops, out, *scratch):
    chunks = len(sizes)
    dbufs, recvs = scratch[:chunks], scratch[chunks : 2 * chunks]
    sends, backs = scratch[2 * chunks : 3 * chunks], scratch[3 * chunks : 4 * chunks]
    apbuf, opsbuf, idbuf, tally = scratch[4 * chunks : 4 * chunks + 4]
    local_sem, recv_sem, send_sem, back_send_sem, back_recv_sem, in_sem, team_sem = scratch[4 * chunks + 4 :]
    me = lax.axis_index("shot")
    parts, team, freqs, shots, traces = data.shape
    plane = team // 2
    total, rows = n * shots, team * shots
    cables = cable_ops.shape[0]
    width = ops.shape[1]
    seat = lax.rem(me, team)
    first = me - seat
    upper = me // team
    spot = lax.rem(me, plane)

    flips = []
    for place in (1 << k for k in range(n.bit_length() - 1)):
        flips.append((place, place * (1 - 2 * lax.rem(me // place, 2))))

    def flip(base, m):
        return base + sum(step for place, step in flips if m & place)

    def signal(sem, device):
        pl.semaphore_signal(sem, inc=1, device_id={"shot": device}, device_id_type=MESH)

    def settle(sem, blocks):
        amount = tally.at[pl.ds(0, blocks)]
        pltpu.make_async_copy(amount, amount, sem).wait()

    offsets = [sum(sizes[:c]) for c in range(chunks)]
    fetches = []
    for c in range(chunks):
        for p in range(parts):
            fetches.append(pltpu.make_async_copy(
                data.at[p, :, pl.ds(offsets[c], sizes[c])],
                dbufs[c].at[:, pl.ds(p * sizes[c], sizes[c])],
                local_sem.at[3 + c * parts + p],
            ))
    fetch_ap = pltpu.make_async_copy(aperture, apbuf, local_sem.at[0])
    fetch_ops = pltpu.make_async_copy(ops, opsbuf, local_sem.at[1])
    fetch_ids = pltpu.make_async_copy(cable_ops, idbuf, local_sem.at[2])
    for fetch in fetches:
        fetch.start()
    fetch_ap.start()

    barrier = pltpu.get_barrier_semaphore()

    @pl.when(upper == 0)
    def _():
        for m in reversed(range(1, n)):
            signal(barrier, flip(me, m))

    fetch_ops.start()
    fetch_ids.start()

    def note():
        fetch_ap.wait()
        lists = apbuf[...]
        surface = lax.broadcasted_iota(jnp.int32, (shots, total), 1)
        found = jnp.zeros((shots, total), jnp.float32)
        for a in range(lists.shape[1]):
            found = jnp.where(lists[:, a : a + 1] == surface, 1.0, found)
        found = found.astype(jnp.bfloat16)
        for k in range(team):
            dbufs[0][k, parts * sizes[0]] = found

    def scatter(c, device, device_seat, near):
        extent = parts * sizes[c] + (c == 0 and near)
        pltpu.make_async_remote_copy(
            src_ref=dbufs[c].at[device_seat, pl.ds(0, extent)],
            dst_ref=recvs[c].at[me, pl.ds(0, extent)],
            send_sem=send_sem.at[c], recv_sem=recv_sem.at[c],
            device_id={"shot": device}, device_id_type=MESH,
        ).start()

    def scatter_near(c):
        for m in reversed(range(1, team)):
            scatter(c, flip(me, m), flip(seat, m), True)
        pltpu.make_async_copy(dbufs[c].at[seat], recvs[c].at[me], recv_sem.at[c]).start()

    level = lax.rem(me // plane, 2)

    def scatter_far(c, *levels):
        low = (1 - upper) * team
        for m in reversed(range(plane)):
            for step in levels:
                place = flip(spot, m) + step * plane
                scatter(c, low + place, place, False)

    @pl.when(upper == 0)
    def _():
        note()
        for fetch in fetches:
            fetch.wait()
        pl.semaphore_wait(barrier, team - 1)
        for c in range(chunks):
            scatter_near(c)
        pl.semaphore_wait(in_sem.at[0], plane)
        scatter_far(0, 0)
        pl.semaphore_wait(in_sem.at[1], plane)

        @pl.when(level == 1)
        def _():
            for step in range(2):
                signal(team_sem, team + step * plane + spot)

        scatter_far(0, 1)
        for c in range(1, chunks):
            scatter_far(c, 1, 0)

    @pl.when(upper == 1)
    def _():
        for fetch in fetches:
            fetch.wait()
        pl.semaphore_wait(barrier, team)

        def announce():
            for m in reversed(range(team, n)):
                signal(in_sem.at[(me - team) // plane], flip(me, m))

        announce()
        for c in range(chunks):
            scatter_far(c, 0, 1)
        note()
        pl.semaphore_wait(team_sem, 1)
        for c in range(chunks):
            scatter_near(c)

    fetch_ops.wait()
    fetch_ids.wait()
    lines = []
    for c in range(cables):
        pieces = [jnp.zeros((width, width), jnp.float32)] * cables
        pieces[c] = opsbuf[idbuf[c]].astype(jnp.float32)
        lines.append(jnp.concatenate(pieces, axis=1))
    operator = jnp.concatenate(lines, axis=0).astype(jnp.bfloat16)

    mask = None
    for c in range(chunks):
        per = sizes[c]
        if c == 0:
            settle(recv_sem.at[0], n * parts * per + team)
        else:
            pltpu.make_async_copy(recvs[c], recvs[c], recv_sem.at[c]).wait()
        if c == 0:
            mask = recvs[0][pl.ds(first, team), parts * per].astype(jnp.float32).reshape(rows, total)
        for f in range(per):
            real = recvs[c][:, f].astype(jnp.float32).reshape(total, traces)
            imag = recvs[c][:, per + f].astype(jnp.float32).reshape(total, traces)
            own_real = recvs[c][pl.ds(first, team), f].astype(jnp.float32).reshape(rows, traces)
            own_imag = recvs[c][pl.ds(first, team), per + f].astype(jnp.float32).reshape(rows, traces)
            left = jnp.concatenate([own_real * mask, own_imag * mask], axis=1).astype(jnp.bfloat16)
            right = jnp.concatenate(
                [jnp.concatenate([real, imag], axis=1), jnp.concatenate([-imag, real], axis=1)], axis=0
            ).astype(jnp.bfloat16)
            product = jnp.dot(left, right, preferred_element_type=jnp.float32)
            product = jnp.concatenate([product[:, :traces], product[:, traces:]], axis=0)
            high = product.astype(jnp.bfloat16)
            rest = product - high.astype(jnp.float32)
            middle = rest.astype(jnp.bfloat16)
            low = (rest - middle.astype(jnp.float32)).astype(jnp.bfloat16)
            result = jnp.dot(low, operator, preferred_element_type=jnp.float32)
            result += jnp.dot(middle, operator, preferred_element_type=jnp.float32)
            result += jnp.dot(high, operator, preferred_element_type=jnp.float32)
            result = result.reshape(parts, team, shots, traces)
            for p in range(parts):
                sends[c][:, p, f] = result[p]

        landing = backs[c].at[seat]
        for m in reversed(range(1, team)):
            pltpu.make_async_remote_copy(
                src_ref=sends[c].at[flip(seat, m)], dst_ref=landing,
                send_sem=back_send_sem.at[c], recv_sem=back_recv_sem.at[c],
                device_id={"shot": flip(me, m)}, device_id_type=MESH,
            ).start()
        pltpu.make_async_copy(sends[c].at[seat], landing, back_recv_sem.at[c]).start()

    for c in range(chunks):
        settle(send_sem.at[c], (n - 1) * parts * sizes[c] + (team - 1) * (c == 0))
    energy = 0.0
    for c in range(chunks):
        pltpu.make_async_copy(backs[c], backs[c], back_recv_sem.at[c]).wait()
        if finish:
            predicted = backs[c][...]
            energy += jnp.sum(predicted * predicted, axis=(0, 1, 2))
    if finish:
        energy = jnp.sum(energy, axis=1, keepdims=True)
        scale = lax.rsqrt(energy / (2.0 * team * freqs * traces) + 1e-06)
    for c in range(chunks):
        for p in range(parts):
            value = backs[c][:, p]
            if finish:
                value = value * scale[None, None]
            out[p, :, pl.ds(offsets[c], sizes[c])] = value.astype(out.dtype)
    for c in range(chunks):
        sent = sends[c].at[pl.ds(0, team - 1)]
        pltpu.make_async_copy(sent, sent, back_send_sem.at[c]).wait()


def per_device(n, bands, data, aperture, ops, cable_ops):
    parts, freqs, shots, traces = data.shape
    team = n // 2
    per = freqs // team
    sizes = [1] * per
    chunks = len(sizes)
    finish = bands == 1
    dma = pltpu.SemaphoreType.DMA
    regular = pltpu.SemaphoreType.REGULAR
    vmem = pltpu.VMEM
    scratch = [vmem((team, parts * s + (c == 0), shots, traces), data.dtype) for c, s in enumerate(sizes)]
    scratch += [vmem((n, parts * s + (c == 0), shots, traces), data.dtype) for c, s in enumerate(sizes)]
    scratch += [vmem((team, parts, s, shots, traces), jnp.float32) for s in sizes] * 2
    scratch += [
        vmem(aperture.shape, aperture.dtype),
        vmem(ops.shape, ops.dtype),
        pltpu.SMEM(cable_ops.shape, cable_ops.dtype),
        vmem((n * parts * max(sizes) + team, shots, traces), data.dtype),
        dma((3 + parts * chunks,)), dma((chunks,)), dma((chunks,)), dma((chunks,)), dma((chunks,)),
        regular((2,)), regular,
    ]
    anywhere = pl.BlockSpec(memory_space=pl.ANY)
    result = pl.pallas_call(
        functools.partial(kernel, n, sizes, finish),
        out_shape=vmem((parts, team, per, shots, traces), jnp.bfloat16 if finish else jnp.float32),
        in_specs=[anywhere] * 4,
        out_specs=pl.BlockSpec(memory_space=vmem),
        scratch_shapes=scratch,
        compiler_params=pltpu.CompilerParams(collective_id=0, has_side_effects=True),
        name="predict",
    )(data.reshape(parts, team, per, shots, traces), aperture, ops, cable_ops)
    result = result.reshape(data.shape)
    if finish:
        return result
    energy = lax.psum(jnp.sum(result * result, axis=(0, 1, 3)), "freq")
    scale = lax.rsqrt(energy / (2.0 * freqs * bands * traces) + 1e-06)
    return (result * scale[None, None, :, None]).astype(jnp.bfloat16)


def solution(mesh):
    return jax.shard_map(
        functools.partial(per_device, mesh.shape["shot"], mesh.shape["freq"]),
        mesh=mesh,
        in_specs=(P(None, "freq", "shot", None), P("shot", None), P(), P()),
        out_specs=P(None, "freq", "shot", None),
        check_vma=False,
    )
```

```python
import functools

import jax
import jax.numpy as jnp
from jax import lax
from jax.experimental import pallas as pl
from jax.experimental.pallas import tpu as pltpu
from jax.sharding import PartitionSpec as P

MESH = pl.DeviceIdType.MESH
PIECES = 2


def kernel(n, sizes, finish, data, aperture, ops, cable_ops, out, *scratch):
    chunks = len(sizes)
    dbufs, recvs = scratch[:chunks], scratch[chunks : 2 * chunks]
    sends, backs = scratch[2 * chunks : 3 * chunks], scratch[3 * chunks : 4 * chunks]
    apbuf, opsbuf, idbuf, lbuf, wbuf, tally = scratch[4 * chunks : 4 * chunks + 6]
    local_sem, recv_sem, send_sem, back_send_sem, back_recv_sem, in_sem, team_sem, group_sem = scratch[4 * chunks + 6 :]
    me = lax.axis_index("shot")
    parts, team, freqs, shots, traces = data.shape
    plane = team // 2
    total, rows = n * shots, team * shots
    cables = cable_ops.shape[0]
    width = ops.shape[1]
    seat = lax.rem(me, team)
    first = me - seat
    upper = me // team
    spot = lax.rem(me, plane)

    flips = []
    for place in (1 << k for k in range(n.bit_length() - 1)):
        flips.append((place, place * (1 - 2 * lax.rem(me // place, 2))))

    def flip(base, m):
        return base + sum(step for place, step in flips if m & place)

    def signal(sem, device):
        pl.semaphore_signal(sem, inc=1, device_id={"shot": device}, device_id_type=MESH)

    def settle_blocks(sem, blocks):
        amount = tally.at[pl.ds(0, blocks)]
        pltpu.make_async_copy(amount, amount, sem).wait()

    def settle(sem, c, near, peers):
        extent = parts * sizes[c] + (c == 0 and near)
        amount = recvs[c].at[pl.ds(0, peers), pl.ds(0, extent)]
        pltpu.make_async_copy(amount, amount, sem).wait()

    offsets = [sum(sizes[:c]) for c in range(chunks)]
    fetches = [
        pltpu.make_async_copy(
            data.at[p, :, pl.ds(offsets[c], sizes[c])],
            dbufs[c].at[:, pl.ds(p * sizes[c], sizes[c])],
            local_sem.at[3],
        )
        for c in range(chunks)
        for p in range(parts)
    ]
    fetch_ap = pltpu.make_async_copy(aperture, apbuf, local_sem.at[0])
    fetch_ops = pltpu.make_async_copy(ops, opsbuf, local_sem.at[1])
    fetch_ids = pltpu.make_async_copy(cable_ops, idbuf, local_sem.at[2])

    barrier = pltpu.get_barrier_semaphore()

    level = lax.rem(me // plane, 2)
    groups = [m for m in range(plane) if not m & 1]

    def opposite(step):
        return (1 - upper) * team + step * plane + spot

    diagonal = groups[-1]

    @pl.when(upper == 0)
    def _():
        for m in sorted(range(1, n), key=lambda m: (m < team, m & diagonal != diagonal, -m)):
            signal(barrier, flip(me, m))

    for fetch in fetches:
        fetch.start()
    fetch_ap.start()

    @pl.when(level * upper == 1)
    def _():
        for step in range(2):
            for m in range(2):
                signal(barrier, flip(opposite(step), m))

    fetch_ops.start()
    fetch_ids.start()

    def note():
        fetch_ap.wait()
        lists = apbuf[...]
        surface = lax.broadcasted_iota(jnp.int32, (shots, total), 1)
        found = jnp.zeros((shots, total), jnp.float32)
        for a in range(lists.shape[1]):
            found = jnp.where(lists[:, a : a + 1] == surface, 1.0, found)
        found = found.astype(jnp.bfloat16)
        for k in range(team):
            dbufs[0][k, parts * sizes[0]] = found

    def scatter(c, device, device_seat, near):
        extent = parts * sizes[c] + (c == 0 and near)
        pltpu.make_async_remote_copy(
            src_ref=dbufs[c].at[device_seat, pl.ds(0, extent)],
            dst_ref=recvs[c].at[me, pl.ds(0, extent)],
            send_sem=send_sem, recv_sem=recv_sem.at[int(near), c],
            device_id={"shot": device}, device_id_type=MESH,
        ).start()

    def scatter_near(c):
        for m in reversed(range(1, team)):
            scatter(c, flip(me, m), flip(seat, m), True)
        pltpu.make_async_copy(dbufs[c].at[seat], recvs[c].at[me], recv_sem.at[1, c]).start()

    def scatter_far(c, *chosen):
        for g in chosen:
            for m in (g + 1, g):
                for step in range(2):
                    place = flip(spot, m) + step * plane
                    scatter(c, (1 - upper) * team + place, place, False)

    @pl.when(upper == 0)
    def _():
        note()
        pltpu.make_async_copy(data, data, local_sem.at[3]).wait()
        pl.semaphore_wait(barrier, team + 1)
        scatter_near(0)
        pl.semaphore_wait(in_sem, 2)
        for g in groups[1:]:
            signal(group_sem.at[g // 2 - 1], flip(me, g))
        for c in range(1, chunks):
            scatter_near(c)
        for c in range(chunks):
            scatter_far(c, 0)
        for g in groups[1:]:
            pl.semaphore_wait(group_sem.at[g // 2 - 1], 1)
            if g == groups[-1]:

                @pl.when(level == 1)
                def _():
                    for step in range(2):
                        signal(team_sem, opposite(step))

            scatter_far(0, g)
        for c in range(1, chunks):
            scatter_far(c, *reversed(groups[1:]))

    @pl.when(upper == 1)
    def _():
        pltpu.make_async_copy(data, data, local_sem.at[3]).wait()
        pl.semaphore_wait(barrier, team)

        @pl.when(level == 0)
        def _():
            for step in range(2):
                for m in range(2):
                    signal(in_sem, flip(opposite(step), m))

        for c in range(chunks - 1):
            scatter_far(c, *reversed(groups))
            if c == 1:
                note()
        if chunks < 3:
            note()
        pl.semaphore_wait(team_sem, 1)
        scatter_near(0)
        scatter_far(chunks - 1, *reversed(groups))
        for c in range(1, chunks):
            scatter_near(c)

    fetch_ops.wait()
    fetch_ids.wait()
    lines = []
    for c in range(cables):
        pieces = [jnp.zeros((width, width), jnp.float32)] * cables
        pieces[c] = opsbuf[idbuf[c]].astype(jnp.float32)
        lines.append(jnp.concatenate(pieces, axis=1))
    operator = jnp.concatenate([jnp.concatenate(lines, axis=0).astype(jnp.bfloat16)] * PIECES, axis=0)

    def flat(c, start, f):
        return recvs[c][pl.ds(start, team), f].astype(jnp.float32).reshape(rows, traces)

    def place(c, start, f, real, imag):
        base = pl.multiple_of(start * shots, rows)
        wbuf[offsets[c] + f, pl.ds(base, rows)] = real.astype(jnp.bfloat16)
        wbuf[offsets[c] + f, pl.ds(base + total, rows)] = imag.astype(jnp.bfloat16)

    masks = []

    def prepare(c):
        per = sizes[c]
        settle(recv_sem.at[1, c], c, True, team)
        if c == 0:
            masks.append(recvs[0][pl.ds(first, team), parts * per].astype(jnp.float32).reshape(rows, total))
        for f in range(per):
            real, imag = flat(c, first, f), flat(c, first, per + f)
            place(c, first, f, real, imag)
            real, imag = real * masks[0], imag * masks[0]
            lbuf[offsets[c] + f] = jnp.concatenate(
                [jnp.concatenate([real, -imag], axis=1), jnp.concatenate([imag, real], axis=1)], axis=0
            ).astype(jnp.bfloat16)

    def finish_chunk(c):
        per = sizes[c]
        settle(recv_sem.at[0, c], c, False, team)
        for f in range(per):
            place(c, team - first, f, flat(c, team - first, f), flat(c, team - first, per + f))
            rest = jnp.dot(lbuf[offsets[c] + f], wbuf[offsets[c] + f], preferred_element_type=jnp.float32)
            pieces = []
            for piece in range(PIECES):
                pieces.append(rest.astype(jnp.bfloat16))
                rest = rest - pieces[-1].astype(jnp.float32)
            result = jnp.dot(jnp.concatenate(pieces[::-1], axis=1), operator, preferred_element_type=jnp.float32)
            result = result.reshape(parts, team, shots, traces)
            for p in range(parts):
                sends[c][:, p, f] = result[p]

        landing = backs[c].at[seat]
        for m in reversed(range(1, team)):
            pltpu.make_async_remote_copy(
                src_ref=sends[c].at[flip(seat, m)], dst_ref=landing,
                send_sem=back_send_sem, recv_sem=back_recv_sem.at[max(0, c + 2 - chunks)],
                device_id={"shot": flip(me, m)}, device_id_type=MESH,
            ).start()
        pltpu.make_async_copy(sends[c].at[seat], landing, back_recv_sem.at[max(0, c + 2 - chunks)]).start()

    for c in range(-2, chunks):
        if c >= 0:
            finish_chunk(c)
        if c + 2 < chunks:
            prepare(c + 2)

    settle_blocks(send_sem, (n - 1) * parts * freqs + team - 1)

    def wait_back(which, c_from, c_to):
        total_f = sum(sizes[c_from:c_to])
        settle_blocks(back_recv_sem.at[which], 2 * team * parts * total_f)

    def power(c):
        predicted = backs[c][...]
        return jnp.sum(predicted * predicted, axis=(0, 1, 2))

    energy = jnp.zeros((shots, traces), jnp.float32)
    if chunks > 1:
        wait_back(0, 0, chunks - 1)
        for c in range(chunks - 1):
            energy += power(c)
    wait_back(1, chunks - 1, chunks)
    energy = jnp.sum(energy + power(chunks - 1), axis=1, keepdims=True)
    scale = lax.rsqrt(energy / (2.0 * team * freqs * traces) + 1e-06)
    for c in range(chunks):
        for p in range(parts):
            value = backs[c][:, p]
            if finish:
                value = value * scale[None, None]
            out[p, :, pl.ds(offsets[c], sizes[c])] = value.astype(out.dtype)
    settle_blocks(back_send_sem, 2 * (team - 1) * parts * freqs)


def per_device(n, bands, data, aperture, ops, cable_ops):
    parts, freqs, shots, traces = data.shape
    team = n // 2
    per = freqs // team
    sizes = [1] * per
    chunks = len(sizes)
    finish = bands == 1
    dma = pltpu.SemaphoreType.DMA
    regular = pltpu.SemaphoreType.REGULAR
    vmem = pltpu.VMEM
    scratch = [vmem((team, parts * s + (c == 0), shots, traces), data.dtype) for c, s in enumerate(sizes)]
    scratch += [vmem((n, parts * s + (c == 0), shots, traces), data.dtype) for c, s in enumerate(sizes)]
    scratch += [vmem((team, parts, s, shots, traces), jnp.float32) for s in sizes] * 2
    scratch += [
        vmem(aperture.shape, aperture.dtype),
        vmem(ops.shape, ops.dtype),
        pltpu.SMEM(cable_ops.shape, cable_ops.dtype),
        vmem((per, parts * team * shots, parts * traces), data.dtype),
        vmem((per, parts * n * shots, traces), data.dtype),
        vmem((n * parts * per + team, shots, traces), data.dtype),
        dma((4,)), dma((2, chunks)), dma, dma, dma((2,)),
        regular, regular, regular((n // 8 - 1,)),
    ]
    anywhere = pl.BlockSpec(memory_space=pl.ANY)
    result = pl.pallas_call(
        functools.partial(kernel, n, sizes, finish),
        out_shape=vmem((parts, team, per, shots, traces), jnp.bfloat16 if finish else jnp.float32),
        in_specs=[anywhere] * 4,
        out_specs=pl.BlockSpec(memory_space=vmem),
        scratch_shapes=scratch,
        compiler_params=pltpu.CompilerParams(collective_id=0, has_side_effects=True),
        name="predict",
    )(data.reshape(parts, team, per, shots, traces), aperture, ops, cable_ops)
    result = result.reshape(data.shape)
    if finish:
        return result
    energy = lax.psum(jnp.sum(result * result, axis=(0, 1, 3)), "freq")
    scale = lax.rsqrt(energy / (2.0 * freqs * bands * traces) + 1e-06)
    return (result * scale[None, None, :, None]).astype(jnp.bfloat16)


def solution(mesh):
    return jax.shard_map(
        functools.partial(per_device, mesh.shape["shot"], mesh.shape["freq"]),
        mesh=mesh,
        in_specs=(P(None, "freq", "shot", None), P("shot", None), P(), P()),
        out_specs=P(None, "freq", "shot", None),
        check_vma=False,
    )
```

```python
import functools

import jax
import jax.numpy as jnp
from jax import lax
from jax.experimental import pallas as pl
from jax.experimental.pallas import tpu as pltpu
from jax.sharding import PartitionSpec as P

MESH = pl.DeviceIdType.MESH
PIECES = 3


def kernel(n, sizes, finish, data, aperture, ops, cable_ops, out, *scratch):
    chunks = len(sizes)
    dbufs, recvs = scratch[:chunks], scratch[chunks : 2 * chunks]
    sends, backs = scratch[2 * chunks : 3 * chunks], scratch[3 * chunks : 4 * chunks]
    apbuf, opsbuf, idbuf, lbuf, wbuf, tally = scratch[4 * chunks : 4 * chunks + 6]
    local_sem, recv_sem, send_sem, back_send_sem, back_recv_sem, in_sem, team_sem, group_sem = scratch[4 * chunks + 6 :]
    me = lax.axis_index("shot")
    parts, team, freqs, shots, traces = data.shape
    plane = team // 2
    total, rows = n * shots, team * shots
    cables = cable_ops.shape[0]
    width = ops.shape[1]
    seat = lax.rem(me, team)
    first = me - seat
    upper = me // team
    spot = lax.rem(me, plane)

    flips = []
    for place in (1 << k for k in range(n.bit_length() - 1)):
        flips.append((place, place * (1 - 2 * lax.rem(me // place, 2))))

    def flip(base, m):
        return base + sum(step for place, step in flips if m & place)

    def signal(sem, device):
        pl.semaphore_signal(sem, inc=1, device_id={"shot": device}, device_id_type=MESH)

    def settle_blocks(sem, blocks):
        amount = tally.at[pl.ds(0, blocks)]
        pltpu.make_async_copy(amount, amount, sem).wait()

    def settle(sem, c, near, peers):
        extent = parts * sizes[c] + (c == 0 and near)
        amount = recvs[c].at[pl.ds(0, peers), pl.ds(0, extent)]
        pltpu.make_async_copy(amount, amount, sem).wait()

    offsets = [sum(sizes[:c]) for c in range(chunks)]
    fetches = [
        pltpu.make_async_copy(
            data.at[p, :, pl.ds(offsets[c], sizes[c])],
            dbufs[c].at[:, pl.ds(p * sizes[c], sizes[c])],
            local_sem.at[3],
        )
        for c in range(chunks)
        for p in range(parts)
    ]
    fetch_ap = pltpu.make_async_copy(aperture, apbuf, local_sem.at[0])
    fetch_ops = pltpu.make_async_copy(ops, opsbuf, local_sem.at[1])
    fetch_ids = pltpu.make_async_copy(cable_ops, idbuf, local_sem.at[2])

    barrier = pltpu.get_barrier_semaphore()

    level = lax.rem(me // plane, 2)
    groups = [m for m in range(plane) if not m & 1]

    def opposite(step):
        return (1 - upper) * team + step * plane + spot

    diagonal = groups[-1]

    @pl.when(upper == 0)
    def _():
        for m in sorted(range(1, n), key=lambda m: (m < team, m & diagonal != diagonal, -m)):
            signal(barrier, flip(me, m))

    for fetch in fetches:
        fetch.start()
    fetch_ap.start()

    @pl.when(level * upper == 1)
    def _():
        for step in range(2):
            for m in range(2):
                signal(barrier, flip(opposite(step), m))

    fetch_ops.start()
    fetch_ids.start()

    def note():
        fetch_ap.wait()
        lists = apbuf[...]
        surface = lax.broadcasted_iota(jnp.int32, (shots, total), 1)
        found = jnp.zeros((shots, total), jnp.float32)
        for a in range(lists.shape[1]):
            found = jnp.where(lists[:, a : a + 1] == surface, 1.0, found)
        found = found.astype(jnp.bfloat16)
        for k in range(team):
            dbufs[0][k, parts * sizes[0]] = found

    def scatter(c, device, device_seat, near):
        extent = parts * sizes[c] + (c == 0 and near)
        pltpu.make_async_remote_copy(
            src_ref=dbufs[c].at[device_seat, pl.ds(0, extent)],
            dst_ref=recvs[c].at[me, pl.ds(0, extent)],
            send_sem=send_sem, recv_sem=recv_sem.at[int(near), c],
            device_id={"shot": device}, device_id_type=MESH,
        ).start()

    def scatter_near(c):
        for m in reversed(range(1, team)):
            scatter(c, flip(me, m), flip(seat, m), True)
        pltpu.make_async_copy(dbufs[c].at[seat], recvs[c].at[me], recv_sem.at[1, c]).start()

    def scatter_far(c, *chosen):
        for g in chosen:
            for m in (g + 1, g):
                for step in range(2):
                    place = flip(spot, m) + step * plane
                    scatter(c, (1 - upper) * team + place, place, False)

    @pl.when(upper == 0)
    def _():
        note()
        pltpu.make_async_copy(data, data, local_sem.at[3]).wait()
        pl.semaphore_wait(barrier, team + 1)
        scatter_near(0)
        pl.semaphore_wait(in_sem, 2)
        for g in groups[1:]:
            signal(group_sem.at[g // 2 - 1], flip(me, g))
        for c in range(1, chunks):
            scatter_near(c)
        for c in range(chunks):
            scatter_far(c, 0)
        for g in groups[1:]:
            pl.semaphore_wait(group_sem.at[g // 2 - 1], 1)
            if g == groups[-1]:

                @pl.when(level == 1)
                def _():
                    for step in range(2):
                        signal(team_sem, opposite(step))

            scatter_far(0, g)
        for c in range(1, chunks):
            scatter_far(c, *reversed(groups[1:]))

    @pl.when(upper == 1)
    def _():
        pltpu.make_async_copy(data, data, local_sem.at[3]).wait()
        pl.semaphore_wait(barrier, team)

        @pl.when(level == 0)
        def _():
            for step in range(2):
                for m in range(2):
                    signal(in_sem, flip(opposite(step), m))

        for c in range(chunks - 1):
            scatter_far(c, *reversed(groups))
            if c == 1:
                note()
        if chunks < 3:
            note()
        pl.semaphore_wait(team_sem, 1)
        scatter_near(0)
        scatter_far(chunks - 1, *reversed(groups))
        for c in range(1, chunks):
            scatter_near(c)

    fetch_ops.wait()
    fetch_ids.wait()
    lines = []
    for c in range(cables):
        pieces = [jnp.zeros((width, width), jnp.float32)] * cables
        pieces[c] = opsbuf[idbuf[c]].astype(jnp.float32)
        lines.append(jnp.concatenate(pieces, axis=1))
    operator = jnp.concatenate([jnp.concatenate(lines, axis=0).astype(jnp.bfloat16)] * PIECES, axis=0)

    def flat(c, start, f):
        return recvs[c][pl.ds(start, team), f].astype(jnp.float32).reshape(rows, traces)

    def place(c, start, f, real, imag):
        base = pl.multiple_of(start * shots, rows)
        wbuf[offsets[c] + f, pl.ds(base, rows)] = real.astype(jnp.bfloat16)
        wbuf[offsets[c] + f, pl.ds(base + total, rows)] = imag.astype(jnp.bfloat16)

    masks = []

    def prepare(c):
        per = sizes[c]
        settle(recv_sem.at[1, c], c, True, team)
        if c == 0:
            masks.append(recvs[0][pl.ds(first, team), parts * per].astype(jnp.float32).reshape(rows, total))
        for f in range(per):
            real, imag = flat(c, first, f), flat(c, first, per + f)
            place(c, first, f, real, imag)
            real, imag = real * masks[0], imag * masks[0]
            lbuf[offsets[c] + f] = jnp.concatenate(
                [jnp.concatenate([real, -imag], axis=1), jnp.concatenate([imag, real], axis=1)], axis=0
            ).astype(jnp.bfloat16)

    def finish_chunk(c):
        per = sizes[c]
        settle(recv_sem.at[0, c], c, False, team)
        for f in range(per):
            place(c, team - first, f, flat(c, team - first, f), flat(c, team - first, per + f))
            rest = jnp.dot(lbuf[offsets[c] + f], wbuf[offsets[c] + f], preferred_element_type=jnp.float32)
            pieces = []
            for piece in range(PIECES):
                pieces.append(rest.astype(jnp.bfloat16))
                rest = rest - pieces[-1].astype(jnp.float32)
            result = jnp.dot(jnp.concatenate(pieces[::-1], axis=1), operator, preferred_element_type=jnp.float32)
            result = result.reshape(parts, team, shots, traces)
            for p in range(parts):
                sends[c][:, p, f] = result[p]

        landing = backs[c].at[seat]
        for m in reversed(range(1, team)):
            pltpu.make_async_remote_copy(
                src_ref=sends[c].at[flip(seat, m)], dst_ref=landing,
                send_sem=back_send_sem, recv_sem=back_recv_sem.at[max(0, c + 2 - chunks)],
                device_id={"shot": flip(me, m)}, device_id_type=MESH,
            ).start()
        pltpu.make_async_copy(sends[c].at[seat], landing, back_recv_sem.at[max(0, c + 2 - chunks)]).start()

    for c in range(-2, chunks):
        if c >= 0:
            finish_chunk(c)
        if c + 2 < chunks:
            prepare(c + 2)

    settle_blocks(send_sem, (n - 1) * parts * freqs + team - 1)

    def wait_back(which, c_from, c_to):
        total_f = sum(sizes[c_from:c_to])
        settle_blocks(back_recv_sem.at[which], 2 * team * parts * total_f)

    def power(c):
        predicted = backs[c][...]
        return jnp.sum(predicted * predicted, axis=(0, 1, 2))

    energy = jnp.zeros((shots, traces), jnp.float32)
    if chunks > 1:
        wait_back(0, 0, chunks - 1)
        for c in range(chunks - 1):
            energy += power(c)
    wait_back(1, chunks - 1, chunks)
    energy = jnp.sum(energy + power(chunks - 1), axis=1, keepdims=True)
    scale = lax.rsqrt(energy / (2.0 * team * freqs * traces) + 1e-06)
    for c in range(chunks):
        for p in range(parts):
            value = backs[c][:, p]
            if finish:
                value = value * scale[None, None]
            out[p, :, pl.ds(offsets[c], sizes[c])] = value.astype(out.dtype)
    settle_blocks(back_send_sem, 2 * (team - 1) * parts * freqs)


def per_device(n, bands, data, aperture, ops, cable_ops):
    parts, freqs, shots, traces = data.shape
    team = n // 2
    per = freqs // team
    sizes = [1] * per
    chunks = len(sizes)
    finish = bands == 1
    dma = pltpu.SemaphoreType.DMA
    regular = pltpu.SemaphoreType.REGULAR
    vmem = pltpu.VMEM
    scratch = [vmem((team, parts * s + (c == 0), shots, traces), data.dtype) for c, s in enumerate(sizes)]
    scratch += [vmem((n, parts * s + (c == 0), shots, traces), data.dtype) for c, s in enumerate(sizes)]
    scratch += [vmem((team, parts, s, shots, traces), jnp.float32) for s in sizes] * 2
    scratch += [
        vmem(aperture.shape, aperture.dtype),
        vmem(ops.shape, ops.dtype),
        pltpu.SMEM(cable_ops.shape, cable_ops.dtype),
        vmem((per, parts * team * shots, parts * traces), data.dtype),
        vmem((per, parts * n * shots, traces), data.dtype),
        vmem((n * parts * per + team, shots, traces), data.dtype),
        dma((4,)), dma((2, chunks)), dma, dma, dma((2,)),
        regular, regular, regular((n // 8 - 1,)),
    ]
    anywhere = pl.BlockSpec(memory_space=pl.ANY)
    result = pl.pallas_call(
        functools.partial(kernel, n, sizes, finish),
        out_shape=vmem((parts, team, per, shots, traces), jnp.bfloat16 if finish else jnp.float32),
        in_specs=[anywhere] * 4,
        out_specs=pl.BlockSpec(memory_space=vmem),
        scratch_shapes=scratch,
        compiler_params=pltpu.CompilerParams(collective_id=0, has_side_effects=True),
        name="predict",
    )(data.reshape(parts, team, per, shots, traces), aperture, ops, cable_ops)
    result = result.reshape(data.shape)
    if finish:
        return result
    energy = lax.psum(jnp.sum(result * result, axis=(0, 1, 3)), "freq")
    scale = lax.rsqrt(energy / (2.0 * freqs * bands * traces) + 1e-06)
    return (result * scale[None, None, :, None]).astype(jnp.bfloat16)


def solution(mesh):
    return jax.shard_map(
        functools.partial(per_device, mesh.shape["shot"], mesh.shape["freq"]),
        mesh=mesh,
        in_specs=(P(None, "freq", "shot", None), P("shot", None), P(), P()),
        out_specs=P(None, "freq", "shot", None),
        check_vma=False,
    )
```

```python
import functools

import jax
import jax.numpy as jnp
from jax import lax
from jax.experimental import pallas as pl
from jax.experimental.pallas import tpu as pltpu
from jax.sharding import PartitionSpec as P

MESH = pl.DeviceIdType.MESH
PIECES = 3


def kernel(n, sizes, finish, data, aperture, ops, cable_ops, out, *scratch):
    chunks = len(sizes)
    dbufs, recvs = scratch[:chunks], scratch[chunks : 2 * chunks]
    sends, backs = scratch[2 * chunks : 3 * chunks], scratch[3 * chunks : 4 * chunks]
    apbuf, opsbuf, idbuf, lbuf, wbuf, tally = scratch[4 * chunks : 4 * chunks + 6]
    local_sem, recv_sem, send_sem, back_send_sem, back_recv_sem, in_sem, col_sem, team_sem, group_sem = scratch[4 * chunks + 6 :]
    me = lax.axis_index("shot")
    parts, team, freqs, shots, traces = data.shape
    plane = team // 2
    total, rows = n * shots, team * shots
    cables = cable_ops.shape[0]
    width = ops.shape[1]
    seat = lax.rem(me, team)
    first = me - seat
    upper = me // team
    spot = lax.rem(me, plane)

    flips = []
    for place in (1 << k for k in range(n.bit_length() - 1)):
        flips.append((place, place * (1 - 2 * lax.rem(me // place, 2))))

    def flip(base, m):
        return base + sum(step for place, step in flips if m & place)

    def signal(sem, device):
        pl.semaphore_signal(sem, inc=1, device_id={"shot": device}, device_id_type=MESH)

    def settle_blocks(sem, blocks):
        amount = tally.at[pl.ds(0, blocks)]
        pltpu.make_async_copy(amount, amount, sem).wait()

    def settle(sem, c, near, peers):
        extent = parts * sizes[c] + (c == 0 and near)
        amount = recvs[c].at[pl.ds(0, peers), pl.ds(0, extent)]
        pltpu.make_async_copy(amount, amount, sem).wait()

    offsets = [sum(sizes[:c]) for c in range(chunks)]
    fetches = [
        pltpu.make_async_copy(
            data.at[p, :, pl.ds(offsets[c], sizes[c])],
            dbufs[c].at[:, pl.ds(p * sizes[c], sizes[c])],
            local_sem.at[3],
        )
        for c in range(chunks)
        for p in range(parts)
    ]
    fetch_ap = pltpu.make_async_copy(aperture, apbuf, local_sem.at[0])
    fetch_ops = pltpu.make_async_copy(ops, opsbuf, local_sem.at[1])
    fetch_ids = pltpu.make_async_copy(cable_ops, idbuf, local_sem.at[2])

    barrier = pltpu.get_barrier_semaphore()

    level = lax.rem(me // plane, 2)
    groups = [m for m in range(plane) if not m & 1]

    def opposite(step):
        return (1 - upper) * team + step * plane + spot

    diagonal = groups[-1]

    @pl.when(upper == 0)
    def _():
        for m in sorted(range(1, n), key=lambda m: (m < team, m & diagonal != diagonal, -m)):
            signal(barrier, flip(me, m))

    for fetch in fetches:
        fetch.start()
    fetch_ap.start()

    @pl.when(level * upper == 1)
    def _():
        for m in range(2):
            signal(barrier, flip(opposite(1), m))

    fetch_ops.start()
    fetch_ids.start()

    def note():
        fetch_ap.wait()
        lists = apbuf[...]
        surface = lax.broadcasted_iota(jnp.int32, (shots, total), 1)
        found = jnp.zeros((shots, total), jnp.float32)
        for a in range(lists.shape[1]):
            found = jnp.where(lists[:, a : a + 1] == surface, 1.0, found)
        found = found.astype(jnp.bfloat16)
        for k in range(team):
            dbufs[0][k, parts * sizes[0]] = found

    def scatter(c, device, device_seat, near):
        extent = parts * sizes[c] + (c == 0 and near)
        pltpu.make_async_remote_copy(
            src_ref=dbufs[c].at[device_seat, pl.ds(0, extent)],
            dst_ref=recvs[c].at[me, pl.ds(0, extent)],
            send_sem=send_sem, recv_sem=recv_sem.at[int(near), c],
            device_id={"shot": device}, device_id_type=MESH,
        ).start()

    def scatter_near(c):
        for m in reversed(range(1, team)):
            scatter(c, flip(me, m), flip(seat, m), True)
        pltpu.make_async_copy(dbufs[c].at[seat], recvs[c].at[me], recv_sem.at[1, c]).start()

    def scatter_far(c, *chosen):
        for g in chosen:
            for m in (g + 1, g):
                for step in range(2):
                    place = flip(spot, m) + step * plane
                    scatter(c, (1 - upper) * team + place, place, False)

    @pl.when(upper == 0)
    def _():
        note()
        pltpu.make_async_copy(data, data, local_sem.at[3]).wait()
        pl.semaphore_wait(barrier, team - 1 + 2 * level)

        @pl.when(level == 1)
        def _():
            signal(col_sem, spot)

        scatter_near(0)
        pl.semaphore_wait(in_sem, 2)

        @pl.when(level == 0)
        def _():
            pl.semaphore_wait(col_sem, 1)

        for g in groups[1:]:
            signal(group_sem.at[g // 2 - 1], flip(me, g))
        for c in range(1, chunks):
            scatter_near(c)
        for c in range(chunks):
            scatter_far(c, 0)
        for g in groups[1:]:
            pl.semaphore_wait(group_sem.at[g // 2 - 1], 1)
            if g == groups[-1]:

                @pl.when(level == 1)
                def _():
                    for step in range(2):
                        signal(team_sem, opposite(step))

            scatter_far(0, g)
        for c in range(1, chunks):
            scatter_far(c, *reversed(groups[1:]))

    @pl.when(upper == 1)
    def _():
        pltpu.make_async_copy(data, data, local_sem.at[3]).wait()
        pl.semaphore_wait(barrier, team)

        @pl.when(level == 0)
        def _():
            for step in range(2):
                for m in range(2):
                    signal(in_sem, flip(opposite(step), m))

        for c in range(chunks - 1):
            scatter_far(c, *reversed(groups))
            if c == 1:
                note()
        if chunks < 3:
            note()
        pl.semaphore_wait(team_sem, 1)
        half = len(groups) // 2
        scatter_near(0)
        scatter_far(chunks - 1, *groups[: half - 1 : -1])
        for c in range(1, min(2, chunks)):
            scatter_near(c)
        scatter_far(chunks - 1, *groups[:half][::-1])
        for c in range(2, chunks):
            scatter_near(c)

    fetch_ops.wait()
    fetch_ids.wait()
    lines = []
    for c in range(cables):
        pieces = [jnp.zeros((width, width), jnp.float32)] * cables
        pieces[c] = opsbuf[idbuf[c]].astype(jnp.float32)
        lines.append(jnp.concatenate(pieces, axis=1))
    operator = jnp.concatenate([jnp.concatenate(lines, axis=0).astype(jnp.bfloat16)] * PIECES, axis=0)

    def flat(c, start, f):
        return recvs[c][pl.ds(start, team), f].astype(jnp.float32).reshape(rows, traces)

    def place(c, start, f, real, imag):
        base = pl.multiple_of(start * shots, rows)
        wbuf[offsets[c] + f, pl.ds(base, rows)] = real.astype(jnp.bfloat16)
        wbuf[offsets[c] + f, pl.ds(base + total, rows)] = imag.astype(jnp.bfloat16)

    masks = []

    def prepare(c):
        per = sizes[c]
        settle(recv_sem.at[1, c], c, True, team)
        if c == 0:
            masks.append(recvs[0][pl.ds(first, team), parts * per].astype(jnp.float32).reshape(rows, total))
        for f in range(per):
            real, imag = flat(c, first, f), flat(c, first, per + f)
            place(c, first, f, real, imag)
            real, imag = real * masks[0], imag * masks[0]
            lbuf[offsets[c] + f] = jnp.concatenate(
                [jnp.concatenate([real, -imag], axis=1), jnp.concatenate([imag, real], axis=1)], axis=0
            ).astype(jnp.bfloat16)

    def finish_chunk(c):
        per = sizes[c]
        settle(recv_sem.at[0, c], c, False, team)
        for f in range(per):
            place(c, team - first, f, flat(c, team - first, f), flat(c, team - first, per + f))
            rest = jnp.dot(lbuf[offsets[c] + f], wbuf[offsets[c] + f], preferred_element_type=jnp.float32)
            pieces = []
            for piece in range(PIECES):
                pieces.append(rest.astype(jnp.bfloat16))
                rest = rest - pieces[-1].astype(jnp.float32)
            result = jnp.dot(jnp.concatenate(pieces[::-1], axis=1), operator, preferred_element_type=jnp.float32)
            result = result.reshape(parts, team, shots, traces)
            for p in range(parts):
                sends[c][:, p, f] = result[p]

        landing = backs[c].at[seat]
        for m in reversed(range(1, team)):
            pltpu.make_async_remote_copy(
                src_ref=sends[c].at[flip(seat, m)], dst_ref=landing,
                send_sem=back_send_sem, recv_sem=back_recv_sem.at[max(0, c + 2 - chunks)],
                device_id={"shot": flip(me, m)}, device_id_type=MESH,
            ).start()
        pltpu.make_async_copy(sends[c].at[seat], landing, back_recv_sem.at[max(0, c + 2 - chunks)]).start()

    for c in range(-2, chunks):
        if c >= 0:
            finish_chunk(c)
        if c + 2 < chunks:
            prepare(c + 2)

    settle_blocks(send_sem, (n - 1) * parts * freqs + team - 1)

    def wait_back(which, c_from, c_to):
        total_f = sum(sizes[c_from:c_to])
        settle_blocks(back_recv_sem.at[which], 2 * team * parts * total_f)

    def power(c):
        predicted = backs[c][...]
        return jnp.sum(predicted * predicted, axis=(0, 1, 2))

    energy = jnp.zeros((shots, traces), jnp.float32)
    if chunks > 1:
        wait_back(0, 0, chunks - 1)
        for c in range(chunks - 1):
            energy += power(c)
    wait_back(1, chunks - 1, chunks)
    energy = jnp.sum(energy + power(chunks - 1), axis=1, keepdims=True)
    scale = lax.rsqrt(energy / (2.0 * team * freqs * traces) + 1e-06)
    for c in range(chunks):
        for p in range(parts):
            value = backs[c][:, p]
            if finish:
                value = value * scale[None, None]
            out[p, :, pl.ds(offsets[c], sizes[c])] = value.astype(out.dtype)
    settle_blocks(back_send_sem, 2 * (team - 1) * parts * freqs)


def per_device(n, bands, data, aperture, ops, cable_ops):
    parts, freqs, shots, traces = data.shape
    team = n // 2
    per = freqs // team
    sizes = [1] * per
    chunks = len(sizes)
    finish = bands == 1
    dma = pltpu.SemaphoreType.DMA
    regular = pltpu.SemaphoreType.REGULAR
    vmem = pltpu.VMEM
    scratch = [vmem((team, parts * s + (c == 0), shots, traces), data.dtype) for c, s in enumerate(sizes)]
    scratch += [vmem((n, parts * s + (c == 0), shots, traces), data.dtype) for c, s in enumerate(sizes)]
    scratch += [vmem((team, parts, s, shots, traces), jnp.float32) for s in sizes] * 2
    scratch += [
        vmem(aperture.shape, aperture.dtype),
        vmem(ops.shape, ops.dtype),
        pltpu.SMEM(cable_ops.shape, cable_ops.dtype),
        vmem((per, parts * team * shots, parts * traces), data.dtype),
        vmem((per, parts * n * shots, traces), data.dtype),
        vmem((n * parts * per + team, shots, traces), data.dtype),
        dma((4,)), dma((2, chunks)), dma, dma, dma((2,)),
        regular, regular, regular, regular((n // 8 - 1,)),
    ]
    anywhere = pl.BlockSpec(memory_space=pl.ANY)
    result = pl.pallas_call(
        functools.partial(kernel, n, sizes, finish),
        out_shape=vmem((parts, team, per, shots, traces), jnp.bfloat16 if finish else jnp.float32),
        in_specs=[anywhere] * 4,
        out_specs=pl.BlockSpec(memory_space=vmem),
        scratch_shapes=scratch,
        compiler_params=pltpu.CompilerParams(collective_id=0, has_side_effects=True),
        name="predict",
    )(data.reshape(parts, team, per, shots, traces), aperture, ops, cable_ops)
    result = result.reshape(data.shape)
    if finish:
        return result
    energy = lax.psum(jnp.sum(result * result, axis=(0, 1, 3)), "freq")
    scale = lax.rsqrt(energy / (2.0 * freqs * bands * traces) + 1e-06)
    return (result * scale[None, None, :, None]).astype(jnp.bfloat16)


def solution(mesh):
    return jax.shard_map(
        functools.partial(per_device, mesh.shape["shot"], mesh.shape["freq"]),
        mesh=mesh,
        in_specs=(P(None, "freq", "shot", None), P("shot", None), P(), P()),
        out_specs=P(None, "freq", "shot", None),
        check_vma=False,
    )
```

```python
import functools

import jax
import jax.numpy as jnp
from jax import lax
from jax.experimental import pallas as pl
from jax.experimental.pallas import tpu as pltpu
from jax.sharding import PartitionSpec as P

MESH = pl.DeviceIdType.MESH
PIECES = 3


def kernel(n, sizes, finish, data, aperture, ops, cable_ops, out, *scratch):
    chunks = len(sizes)
    dbufs, recvs = scratch[:chunks], scratch[chunks : 2 * chunks]
    sends, backs = scratch[2 * chunks : 3 * chunks], scratch[3 * chunks : 4 * chunks]
    apbuf, opsbuf, idbuf, lbuf, wbuf, tally = scratch[4 * chunks : 4 * chunks + 6]
    local_sem, recv_sem, send_sem, back_send_sem, back_recv_sem, in_sem, col_sem, team_sem, group_sem = scratch[4 * chunks + 6 :]
    me = lax.axis_index("shot")
    parts, team, freqs, shots, traces = data.shape
    plane = team // 2
    total, rows = n * shots, team * shots
    cables = cable_ops.shape[0]
    width = ops.shape[1]
    seat = lax.rem(me, team)
    first = me - seat
    upper = me // team
    spot = lax.rem(me, plane)

    flips = []
    for place in (1 << k for k in range(n.bit_length() - 1)):
        flips.append((place, place * (1 - 2 * lax.rem(me // place, 2))))

    def flip(base, m):
        return base + sum(step for place, step in flips if m & place)

    def signal(sem, device):
        pl.semaphore_signal(sem, inc=1, device_id={"shot": device}, device_id_type=MESH)

    def settle_blocks(sem, blocks):
        amount = tally.at[pl.ds(0, blocks)]
        pltpu.make_async_copy(amount, amount, sem).wait()

    def settle(sem, c, near, peers):
        extent = parts * sizes[c] + (c == 0 and near)
        amount = recvs[c].at[pl.ds(0, peers), pl.ds(0, extent)]
        pltpu.make_async_copy(amount, amount, sem).wait()

    offsets = [sum(sizes[:c]) for c in range(chunks)]
    fetches = [
        pltpu.make_async_copy(
            data.at[p, :, pl.ds(offsets[c], sizes[c])],
            dbufs[c].at[:, pl.ds(p * sizes[c], sizes[c])],
            local_sem.at[3],
        )
        for c in range(chunks)
        for p in range(parts)
    ]
    fetch_ap = pltpu.make_async_copy(aperture, apbuf, local_sem.at[0])
    fetch_ops = pltpu.make_async_copy(ops, opsbuf, local_sem.at[1])
    fetch_ids = pltpu.make_async_copy(cable_ops, idbuf, local_sem.at[2])

    barrier = pltpu.get_barrier_semaphore()

    level = lax.rem(me // plane, 2)
    groups = [m for m in range(plane) if not m & 1]

    def opposite(step):
        return (1 - upper) * team + step * plane + spot

    diagonal = groups[-1]

    @pl.when(upper == 0)
    def _():
        for m in sorted(range(1, n), key=lambda m: (m < team, m & diagonal != diagonal, -m)):
            signal(barrier, flip(me, m))

    for fetch in fetches:
        fetch.start()
    fetch_ap.start()

    @pl.when(level * upper == 1)
    def _():
        for m in range(2):
            signal(barrier, flip(opposite(1), m))

    fetch_ops.start()
    fetch_ids.start()

    def note():
        fetch_ap.wait()
        lists = apbuf[...]
        surface = lax.broadcasted_iota(jnp.int32, (shots, total), 1)
        found = jnp.zeros((shots, total), jnp.float32)
        for a in range(lists.shape[1]):
            found = jnp.where(lists[:, a : a + 1] == surface, 1.0, found)
        found = found.astype(jnp.bfloat16)
        for k in range(team):
            dbufs[0][k, parts * sizes[0]] = found

    def scatter(c, device, device_seat, near):
        extent = parts * sizes[c] + (c == 0 and near)
        pltpu.make_async_remote_copy(
            src_ref=dbufs[c].at[device_seat, pl.ds(0, extent)],
            dst_ref=recvs[c].at[me, pl.ds(0, extent)],
            send_sem=send_sem, recv_sem=recv_sem.at[int(near), c],
            device_id={"shot": device}, device_id_type=MESH,
        ).start()

    def scatter_near(c):
        for m in reversed(range(1, team)):
            scatter(c, flip(me, m), flip(seat, m), True)
        pltpu.make_async_copy(dbufs[c].at[seat], recvs[c].at[me], recv_sem.at[1, c]).start()

    def scatter_far(c, *chosen):
        for g in chosen:
            for m in (g + 1, g):
                for step in range(2):
                    place = flip(spot, m) + step * plane
                    scatter(c, (1 - upper) * team + place, place, False)

    @pl.when(upper == 0)
    def _():
        note()
        pltpu.make_async_copy(data, data, local_sem.at[3]).wait()
        pl.semaphore_wait(barrier, team - 1 + 2 * level)

        @pl.when(level == 1)
        def _():
            signal(col_sem, spot)

        scatter_near(0)
        pl.semaphore_wait(in_sem, 2)

        @pl.when(level == 0)
        def _():
            pl.semaphore_wait(col_sem, 1)

        for g in groups[1:]:
            signal(group_sem.at[g // 2 - 1], flip(me, g))
        for c in range(1, chunks):
            scatter_near(c)
        for c in range(chunks):
            scatter_far(c, 0)
        for g in groups[1:]:
            pl.semaphore_wait(group_sem.at[g // 2 - 1], 1)
            if g == groups[-1]:

                @pl.when(level == 1)
                def _():
                    for step in range(2):
                        signal(team_sem, opposite(step))

            scatter_far(0, g)
        for c in range(1, chunks):
            scatter_far(c, *reversed(groups[1:]))

    @pl.when(upper == 1)
    def _():
        pltpu.make_async_copy(data, data, local_sem.at[3]).wait()
        pl.semaphore_wait(barrier, team)

        @pl.when(level == 0)
        def _():
            for step in range(2):
                for m in range(2):
                    signal(in_sem, flip(opposite(step), m))

        for c in range(chunks - 1):
            scatter_far(c, *reversed(groups))
            if c == 0:
                note()
        if chunks < 2:
            note()
        pl.semaphore_wait(team_sem, 1)
        half = len(groups) // 2
        scatter_near(0)
        scatter_far(chunks - 1, *groups[: half - 1 : -1])
        for c in range(1, min(2, chunks)):
            scatter_near(c)
        scatter_far(chunks - 1, *groups[:half][::-1])
        for c in range(2, chunks):
            scatter_near(c)

    fetch_ops.wait()
    fetch_ids.wait()
    lines = []
    for c in range(cables):
        pieces = [jnp.zeros((width, width), jnp.float32)] * cables
        pieces[c] = opsbuf[idbuf[c]].astype(jnp.float32)
        lines.append(jnp.concatenate(pieces, axis=1))
    operator = jnp.concatenate([jnp.concatenate(lines, axis=0).astype(jnp.bfloat16)] * PIECES, axis=0)

    def flat(c, start, f):
        return recvs[c][pl.ds(start, team), f].astype(jnp.float32).reshape(rows, traces)

    def place(c, start, f, real, imag):
        base = pl.multiple_of(start * shots, rows)
        wbuf[offsets[c] + f, pl.ds(base, rows)] = real.astype(jnp.bfloat16)
        wbuf[offsets[c] + f, pl.ds(base + total, rows)] = imag.astype(jnp.bfloat16)

    masks = []

    def prepare(c):
        per = sizes[c]
        settle(recv_sem.at[1, c], c, True, team)
        if c == 0:
            masks.append(recvs[0][pl.ds(first, team), parts * per].astype(jnp.float32).reshape(rows, total))
        for f in range(per):
            real, imag = flat(c, first, f), flat(c, first, per + f)
            place(c, first, f, real, imag)
            real, imag = real * masks[0], imag * masks[0]
            lbuf[offsets[c] + f] = jnp.concatenate(
                [jnp.concatenate([real, -imag], axis=1), jnp.concatenate([imag, real], axis=1)], axis=0
            ).astype(jnp.bfloat16)

    def finish_chunk(c):
        per = sizes[c]
        settle(recv_sem.at[0, c], c, False, team)
        for f in range(per):
            place(c, team - first, f, flat(c, team - first, f), flat(c, team - first, per + f))
            rest = jnp.dot(lbuf[offsets[c] + f], wbuf[offsets[c] + f], preferred_element_type=jnp.float32)
            pieces = []
            for piece in range(PIECES):
                pieces.append(rest.astype(jnp.bfloat16))
                rest = rest - pieces[-1].astype(jnp.float32)
            result = jnp.dot(jnp.concatenate(pieces[::-1], axis=1), operator, preferred_element_type=jnp.float32)
            result = result.reshape(parts, team, shots, traces)
            for p in range(parts):
                sends[c][:, p, f] = result[p]

        landing = backs[c].at[seat]
        for m in reversed(range(1, team)):
            pltpu.make_async_remote_copy(
                src_ref=sends[c].at[flip(seat, m)], dst_ref=landing,
                send_sem=back_send_sem, recv_sem=back_recv_sem.at[max(0, c + 2 - chunks)],
                device_id={"shot": flip(me, m)}, device_id_type=MESH,
            ).start()
        pltpu.make_async_copy(sends[c].at[seat], landing, back_recv_sem.at[max(0, c + 2 - chunks)]).start()

    for c in range(-2, chunks):
        if c >= 0:
            finish_chunk(c)
        if c + 2 < chunks:
            prepare(c + 2)

    settle_blocks(send_sem, (n - 1) * parts * freqs + team - 1)

    def wait_back(which, c_from, c_to):
        total_f = sum(sizes[c_from:c_to])
        settle_blocks(back_recv_sem.at[which], 2 * team * parts * total_f)

    def power(c):
        predicted = backs[c][...]
        return jnp.sum(predicted * predicted, axis=(0, 1, 2))

    energy = jnp.zeros((shots, traces), jnp.float32)
    if chunks > 1:
        wait_back(0, 0, chunks - 1)
        for c in range(chunks - 1):
            energy += power(c)
    wait_back(1, chunks - 1, chunks)
    energy = jnp.sum(energy + power(chunks - 1), axis=1, keepdims=True)
    scale = lax.rsqrt(energy / (2.0 * team * freqs * traces) + 1e-06)
    for c in range(chunks):
        for p in range(parts):
            value = backs[c][:, p]
            if finish:
                value = value * scale[None, None]
            out[p, :, pl.ds(offsets[c], sizes[c])] = value.astype(out.dtype)
    settle_blocks(back_send_sem, 2 * (team - 1) * parts * freqs)


def per_device(n, bands, data, aperture, ops, cable_ops):
    parts, freqs, shots, traces = data.shape
    team = n // 2
    per = freqs // team
    sizes = [1] * per
    chunks = len(sizes)
    finish = bands == 1
    dma = pltpu.SemaphoreType.DMA
    regular = pltpu.SemaphoreType.REGULAR
    vmem = pltpu.VMEM
    scratch = [vmem((team, parts * s + (c == 0), shots, traces), data.dtype) for c, s in enumerate(sizes)]
    scratch += [vmem((n, parts * s + (c == 0), shots, traces), data.dtype) for c, s in enumerate(sizes)]
    scratch += [vmem((team, parts, s, shots, traces), jnp.float32) for s in sizes] * 2
    scratch += [
        vmem(aperture.shape, aperture.dtype),
        vmem(ops.shape, ops.dtype),
        pltpu.SMEM(cable_ops.shape, cable_ops.dtype),
        vmem((per, parts * team * shots, parts * traces), data.dtype),
        vmem((per, parts * n * shots, traces), data.dtype),
        vmem((n * parts * per + team, shots, traces), data.dtype),
        dma((4,)), dma((2, chunks)), dma, dma, dma((2,)),
        regular, regular, regular, regular((n // 8 - 1,)),
    ]
    anywhere = pl.BlockSpec(memory_space=pl.ANY)
    result = pl.pallas_call(
        functools.partial(kernel, n, sizes, finish),
        out_shape=vmem((parts, team, per, shots, traces), jnp.bfloat16 if finish else jnp.float32),
        in_specs=[anywhere] * 4,
        out_specs=pl.BlockSpec(memory_space=vmem),
        scratch_shapes=scratch,
        compiler_params=pltpu.CompilerParams(collective_id=0, has_side_effects=True),
        name="predict",
    )(data.reshape(parts, team, per, shots, traces), aperture, ops, cable_ops)
    result = result.reshape(data.shape)
    if finish:
        return result
    energy = lax.psum(jnp.sum(result * result, axis=(0, 1, 3)), "freq")
    scale = lax.rsqrt(energy / (2.0 * freqs * bands * traces) + 1e-06)
    return (result * scale[None, None, :, None]).astype(jnp.bfloat16)


def solution(mesh):
    return jax.shard_map(
        functools.partial(per_device, mesh.shape["shot"], mesh.shape["freq"]),
        mesh=mesh,
        in_specs=(P(None, "freq", "shot", None), P("shot", None), P(), P()),
        out_specs=P(None, "freq", "shot", None),
        check_vma=False,
    )
```
